256 devices in a mesh: head: 8 (over z_lo, y), tok: 32 (over x, z_hi, core).
Axes of the slice: x: 4, y: 4, z: 8 (z_hi: 4, z_lo: 2; z = z_hi * 2 + z_lo), core: 2. Of those that a mesh axis runs over, the one named last changes fastest.
Arguments:
- queries: bfloat16 [2, 16, 8192, 256], P(None, 'head', 'tok'), may hold values from -6 to 6
- key_vectors: bfloat16 [2, 16, 8192, 256], P(None, 'head', 'tok'), may hold values from -6 to 6
- value_vectors: bfloat16 [2, 16, 8192, 256], P(None, 'head', 'tok'), may hold values from -6 to 6
- step_rates: bfloat16 [2, 16, 8192], P(None, 'head', 'tok'), may hold values from 0.029907227 to 0.29882812
- counts: int32 [2, 32], replicated, may hold values from 1 to 256, 5120 in all within a row
- out_gain: float32 [16, 256], P('head'), may hold values from 0.25 to 1.75
- w_gate: float32 [16, 512, 256], P('head', 'tok'), may hold values from -0.375 to 0.375
- w_up: float32 [16, 512, 256], P('head', 'tok'), may hold values from -0.375 to 0.375
- w_down: float32 [16, 256, 512], P('head', 'tok'), may hold values from -0.25 to 0.25
Outputs:
- mixed_out: bfloat16 [2, 16, 8192, 256], P(None, 'head', 'tok')
- final_gate: float32 [16, 512, 256], P('head', 'tok')
- final_up: float32 [16, 512, 256], P('head', 'tok')
- final_down: float32 [16, 256, 512], P('head', 'tok')
The draws below stay inside these ranges and needn't reach their ends.
Inputs may be any that keep to these rules, and one draw needn't show every extreme that they name: `counts`: the valid tokens are the first ones of each block of 256; each row sums to 256 * 32 * 5 // 8 and some block of each group is full.
All inputs are finite; a program needn't handle non-finite values.
Results may differ from the reference program's by a relative error of at most 0.011.
Values may be sent and summed in bfloat16 or wider, within the bound.
No kernel may reach another device: no remote copies, remote signals or barrier semaphores. Data moves between devices by JAX's collectives and lax.ppermute only.
A program may use at most 64 MiB of HBM per device.

```python
import math
import jax
import jax.numpy as jnp
import numpy as np
from jax import lax

HEADS = 16
DH = 256
FH = 512
BLK = 256
GROUPS = 2
TOKENS = 8192
N_TOK = 32


def level_of(stream_key, dims, split, low, top_value):
    def one(dim, parts):
        heights = jax.random.uniform(jax.random.fold_in(jax.random.fold_in(stream_key, 6), dim), (parts,), jnp.float32, low / len(split), top_value / len(split))
        return jnp.repeat(jnp.exp(heights), dims[dim] // parts).reshape((-1,) + (1,) * (len(dims) - dim - 1))

    gain = one(*split[0])
    for cut in split[1:]:
        gain = gain * one(*cut)
    return gain


def profile(count, total, limit, skew):
    loads = [(1 << 20) // math.isqrt(standing ** skew) + 1 for standing in range(2, count + 1)]
    spare, given = total - limit - (count - 1), [1] * (count - 1)
    while spare > 0:
        movable = [i for i in range(count - 1) if given[i] < limit]
        pool, left = sum([loads[i] for i in movable]), spare
        for i in movable:
            extra = min(limit - given[i], max(1, left * loads[i] // pool), spare)
            given[i] = given[i] + extra
            spare = spare - extra
    return np.array([limit] + given)


def ragged_sizes(key, count, total, bound, lean):
    if count == 2:
        one = jax.random.randint(key, (), max(1, total - bound), min(bound, total - 1) + 1)
        return jnp.stack([one, total - one])
    sizes = jnp.asarray(profile(count, total, bound, lean), jnp.int32)
    twos = (count - 1) // 2
    source_of, sink = sizes[1:1 + 2 * twos:2], sizes[2:2 + 2 * twos:2]
    slack = jnp.minimum(source_of - 1, bound - sink)
    passed = jax.random.randint(jax.random.fold_in(key, 1), (twos,), 0, 1 << 20) % (slack + 1)
    sizes = sizes.at[1:1 + 2 * twos:2].set(source_of - passed).at[2:2 + 2 * twos:2].set(sink + passed)
    return sizes[jax.random.permutation(jax.random.fold_in(key, 2), count)]


def gaussian(own_key, extent, spread, most, cuts=(), kind=jnp.bfloat16):
    array = spread * jax.random.normal(own_key, extent, jnp.float32)
    if cuts:
        array = array * level_of(own_key, extent, cuts, -0.22, 0.18)
    return jnp.clip(array, -most, most).astype(kind)


def setup_inputs(seed: int = 0) -> dict:
    keys = jax.random.split(jax.random.key(seed), 10)
    return {
        "queries": gaussian(keys[0], (GROUPS, HEADS, TOKENS, DH), 1.0, 6.0, ((1, 8), (2, 32))),
        "key_vectors": gaussian(keys[1], (GROUPS, HEADS, TOKENS, DH), 1.0, 6.0, ((1, 8), (2, 32))),
        "value_vectors": gaussian(keys[2], (GROUPS, HEADS, TOKENS, DH), 1.0, 6.0, ((1, 8), (2, 32))),
        "step_rates": jnp.clip(jnp.exp(math.log(0.29882812) - 2.30176843 * jax.random.uniform(keys[3], (GROUPS, HEADS, TOKENS), jnp.float32) ** level_of(keys[3], (GROUPS, HEADS, TOKENS), ((1, 8), (2, 32)), -0.2, 0.2)), 0.029907227, 0.29882812).astype(jnp.bfloat16),
        "counts": jax.vmap(lambda own: ragged_sizes(own, N_TOK, BLK * N_TOK * 5 // 8, BLK, 2))(jax.random.split(keys[4], GROUPS)).reshape((GROUPS, N_TOK)).astype(jnp.int32),
        "out_gain": jnp.clip(1.0 + 0.15 * jax.random.normal(keys[5], (HEADS, DH), jnp.float32), 0.25, 1.75),
        "w_gate": gaussian(keys[6], (HEADS, FH, DH), DH ** -0.5, 0.375, ((0, 8), (1, 32)), jnp.float32),
        "w_up": gaussian(keys[7], (HEADS, FH, DH), DH ** -0.5, 0.375, ((0, 8), (1, 32)), jnp.float32),
        "w_down": gaussian(keys[8], (HEADS, DH, FH), FH ** -0.5, 0.25, ((0, 8), (1, 32)), jnp.float32),
    }


epsilon = 1e-06

def renorm(previous, stepped):
    kept_norm = jnp.sqrt(lax.optimization_barrier(jnp.mean(previous * previous, axis=-1, keepdims=True)))
    return stepped * kept_norm * lax.rsqrt(lax.optimization_barrier(jnp.mean(stepped * stepped, axis=-1, keepdims=True)) + epsilon)

def reference(queries, key_vectors, value_vectors, step_rates, counts, out_gain, w_gate, w_up, w_down):
    grad_scale = float(TOKENS) ** (-0.5)
    positions = jnp.arange(TOKENS, dtype=jnp.int32)
    masters = (w_gate, w_up, w_down)
    outputs = []
    for group in range(GROUPS):
        limits = jnp.take(counts[group], positions // BLK)
        valid_mask = (positions % BLK < limits).astype(jnp.float32)
        fast = tuple((weight_set.astype(jnp.bfloat16) for weight_set in masters))

        def update_head(items):
            gate_w, up_w, down_w, key_rows, value_rows, rate_rows = items
            gate_pre = jnp.dot(key_rows, gate_w.T, preferred_element_type=jnp.float32)
            up_pre = jnp.dot(key_rows, up_w.T, preferred_element_type=jnp.float32)
            sigmoid_gate = jax.nn.sigmoid(gate_pre)
            activated = gate_pre * sigmoid_gate
            hidden = (activated * up_pre).astype(jnp.bfloat16)
            weighted = (value_rows.astype(jnp.float32) * (rate_rows.astype(jnp.float32) * grad_scale * valid_mask)[:, None]).astype(jnp.bfloat16)
            back = jnp.dot(weighted, down_w, preferred_element_type=jnp.float32)
            grad_gate = (back * up_pre * sigmoid_gate * (1.0 + gate_pre * (1.0 - sigmoid_gate))).astype(jnp.bfloat16)
            grad_up = (back * activated).astype(jnp.bfloat16)
            upd_gate = jnp.dot(grad_gate.T, key_rows, preferred_element_type=jnp.float32)
            upd_up = jnp.dot(grad_up.T, key_rows, preferred_element_type=jnp.float32)
            upd_down = jnp.dot(weighted.T, hidden, preferred_element_type=jnp.float32)
            return (upd_gate, upd_up, upd_down)
        updates = lax.map(update_head, (fast[0], fast[1], fast[2], key_vectors[group], value_vectors[group], step_rates[group]))
        masters = tuple((renorm(previous, previous + update) for previous, update in zip(masters, updates)))
        fast = tuple((weight_set.astype(jnp.bfloat16) for weight_set in masters))

        def apply_head(items):
            gate_w, up_w, down_w, query_rows = items
            gate_pre = jnp.dot(query_rows, gate_w.T, preferred_element_type=jnp.float32)
            up_pre = jnp.dot(query_rows, up_w.T, preferred_element_type=jnp.float32)
            hidden = (gate_pre * jax.nn.sigmoid(gate_pre) * up_pre).astype(jnp.bfloat16)
            return jnp.dot(hidden, down_w.T, preferred_element_type=jnp.float32) * valid_mask[:, None]
        heads_out = lax.map(apply_head, (fast[0], fast[1], fast[2], queries[group]))
        mean_square = lax.optimization_barrier(jnp.sum(heads_out * heads_out, axis=(0, 2))) / (HEADS * DH)
        normed = (heads_out * out_gain[:, None, :] * lax.rsqrt(mean_square + epsilon)[None, :, None]).astype(jnp.bfloat16)
        outputs.append(normed)
    return (jnp.stack(outputs), masters[0], masters[1], masters[2])
```

```python
import functools

import jax
import jax.numpy as jnp
from jax import lax
from jax.experimental import pallas as pl
from jax.experimental.pallas import tpu as pltpu
from jax.sharding import Mesh, PartitionSpec as P

HEADS = 16
DH = 256
FH = 512
BLK = 256
EPS = 1e-06
NX = 4
NZ = 4
ROWS = 96

VMEM = pl.BlockSpec(memory_space=pltpu.VMEM)
SMEM = pl.BlockSpec(memory_space=pltpu.SMEM)
NT = (((1,), (1,)), ((), ()))
NN = (((1,), (0,)), ((), ()))
f32 = jnp.float32
bf16 = jnp.bfloat16


def rot(n, d):
    return [(i, (i + d) % n) for i in range(n)]


SWAP = [(0, 1), (1, 0)]


def mm(a, b, dims=NN):
    return lax.dot_general(a, b, dims, preferred_element_type=f32)


def assemble(pos, stacks, g_ref, u_ref, d_ref):
    for dx in range(NX):
        for dz in range(NZ):
            p = lax.rem(pos[0] + (NX - dx), NX) * NZ + lax.rem(pos[1] + (NZ - dz), NZ)
            f0 = pl.multiple_of(p * 32, 32)
            d0 = pl.multiple_of(p * 16, 16)
            g_ref[pl.ds(f0, 32), :] = stacks[dx][dz, 0:32, :]
            u_ref[pl.ds(f0, 32), :] = stacks[dx][dz, 32:64, :]
            d_ref[pl.ds(d0, 16), 0:256] = stacks[dx][dz, 64:80, :]
            d_ref[pl.ds(d0, 16), 256:512] = stacks[dx][dz, 80:96, :]


def update_kernel(
    pos, s0, s1, s2, s3, ko, kr, eo, er, own, o1, o2, o3,
    g_ref, u_ref, d_ref, dt_ref, k_ref, e_ref, et_ref, dg_ref, du_ref, dd_ref,
):
    assemble(pos, (s0, s1, s2, s3), g_ref, u_ref, d_ref)
    k_ref[0:BLK, :] = ko[...].reshape(BLK, DH)
    k_ref[BLK:, :] = kr[...].reshape(BLK, DH)
    e_ref[0:BLK, :] = eo[...].reshape(BLK, DH)
    e_ref[BLK:, :] = er[...].reshape(BLK, DH)
    dt_ref[...] = d_ref[...].T
    et_ref[...] = e_ref[...].T
    step = 128
    for i in range(FH // step):
        rows = slice(i * step, (i + 1) * step)
        a = mm(g_ref[rows, :], k_ref[...], NT)
        b = mm(u_ref[rows, :], k_ref[...], NT)
        r = mm(dt_ref[rows, :], e_ref[...], NT)
        s = jax.nn.sigmoid(a)
        act = a * s
        hid = (act * b).astype(bf16)
        da = (r * b * s * (1.0 + a * (1.0 - s))).astype(bf16)
        db = (r * act).astype(bf16)
        dg_ref[rows, :] = mm(da, k_ref[...])
        du_ref[rows, :] = mm(db, k_ref[...])
        dd_ref[:, rows] = mm(et_ref[...], hid, NT)
    for dx, out in enumerate((own, o1, o2, o3)):
        for dz in range(NZ):
            p = lax.rem(pos[0] + dx, NX) * NZ + lax.rem(pos[1] + dz, NZ)
            f0 = pl.multiple_of(p * 32, 32)
            d0 = pl.multiple_of(p * 16, 16)
            out[dz, 0:32, :] = dg_ref[pl.ds(f0, 32), :].astype(out.dtype)
            out[dz, 32:64, :] = du_ref[pl.ds(f0, 32), :].astype(out.dtype)
            out[dz, 64:80, :] = dd_ref[pl.ds(d0, 16), 0:256].astype(out.dtype)
            out[dz, 80:96, :] = dd_ref[pl.ds(d0, 16), 256:512].astype(out.dtype)


def update(pos, stacks, ko, kr, eo, er):
    return pl.pallas_call(
        update_kernel,
        name="update",
        in_specs=[SMEM] + [VMEM] * 8,
        out_specs=[VMEM] * 4,
        out_shape=[jax.ShapeDtypeStruct((NZ, ROWS, DH), f32)]
        + [jax.ShapeDtypeStruct((NZ, ROWS, DH), bf16)] * 3,
        scratch_shapes=[
            pltpu.VMEM((FH, DH), bf16),
            pltpu.VMEM((FH, DH), bf16),
            pltpu.VMEM((DH, FH), bf16),
            pltpu.VMEM((FH, DH), bf16),
            pltpu.VMEM((2 * BLK, DH), bf16),
            pltpu.VMEM((2 * BLK, DH), bf16),
            pltpu.VMEM((DH, 2 * BLK), bf16),
            pltpu.VMEM((FH, DH), f32),
            pltpu.VMEM((FH, DH), f32),
            pltpu.VMEM((DH, FH), f32),
        ],
    )(pos, *stacks, ko, kr, eo, er)


def partial_kernel(own, r1, r2, r3, y0, y1, y2, y3):
    for dz, out in enumerate((y0, y1, y2, y3)):
        total = own[dz] + r1[dz].astype(f32) + r2[dz].astype(f32) + r3[dz].astype(f32)
        out[...] = total.astype(out.dtype)


def partial_sum(own, recv):
    return pl.pallas_call(
        partial_kernel,
        name="partial_sum",
        in_specs=[VMEM] * 4,
        out_specs=[VMEM] * 4,
        out_shape=[jax.ShapeDtypeStruct((ROWS, DH), f32)]
        + [jax.ShapeDtypeStruct((ROWS, DH), bf16)] * 3,
    )(own, *recv)


def renorm_kernel(w, y0, t1, t2, t3, w_out, piece):
    old = w[...]
    new = old + (y0[...] + t1[...].astype(f32) + t2[...].astype(f32) + t3[...].astype(f32))

    def mean_square(v):
        sums = jnp.sum(v * v, axis=-1, keepdims=True)
        wide = (sums[64:80] + sums[80:96]) * (1.0 / FH)
        return jnp.concatenate([sums[0:64] * (1.0 / DH), wide, wide], axis=0)

    scaled = new * jnp.sqrt(mean_square(old)) * lax.rsqrt(mean_square(new) + EPS)
    w_out[...] = scaled
    piece[...] = scaled.astype(bf16)


def renorm(w, y0, recv):
    return pl.pallas_call(
        renorm_kernel,
        name="renorm",
        in_specs=[VMEM] * 5,
        out_specs=[VMEM] * 2,
        out_shape=[
            jax.ShapeDtypeStruct((ROWS, DH), f32),
            jax.ShapeDtypeStruct((ROWS, DH), bf16),
        ],
    )(w, y0, *recv)


def apply_kernel(
    pos, s0, s1, s2, s3, qo, qr, o_own, o_send, sq_own, sq_send, g_ref, u_ref, d_ref
):
    assemble(pos, (s0, s1, s2, s3), g_ref, u_ref, d_ref)
    for which, (q, out, sq) in enumerate(((qo, o_own, sq_own), (qr, o_send, sq_send))):
        query = q[...].reshape(BLK, DH)
        a = mm(query, g_ref[...], NT)
        b = mm(query, u_ref[...], NT)
        hid = (a * jax.nn.sigmoid(a) * b).astype(bf16)
        o = mm(hid, d_ref[...], NT)
        valid = lax.broadcasted_iota(jnp.int32, (BLK, DH), 0) < pos[2 + which]
        o = jnp.where(valid, o, 0.0)
        out[...] = o.astype(out.dtype)
        sums = jnp.sum(o * o, axis=-1, keepdims=True)
        sq[...] = jnp.broadcast_to(sums, (BLK, 128)).T[0:8, :]


def apply(pos, stacks, qo, qr):
    return pl.pallas_call(
        apply_kernel,
        name="apply",
        in_specs=[SMEM] + [VMEM] * 6,
        out_specs=[VMEM] * 4,
        out_shape=[
            jax.ShapeDtypeStruct((BLK, DH), f32),
            jax.ShapeDtypeStruct((BLK, DH), bf16),
            jax.ShapeDtypeStruct((8, BLK), f32),
            jax.ShapeDtypeStruct((8, BLK), f32),
        ],
        scratch_shapes=[
            pltpu.VMEM((FH, DH), bf16),
            pltpu.VMEM((FH, DH), bf16),
            pltpu.VMEM((DH, FH), bf16),
        ],
    )(pos, *stacks, qo, qr)


def finish_kernel(core, gain, o0, r0, q0, o1, r1, q1, out):
    c = core[0]
    for g, (o, r, q) in enumerate(((o0, r0, q0), (o1, r1, q1))):
        row = lax.rsqrt(q[0:1, :] * (1.0 / (HEADS * DH)) + EPS)
        scale = jnp.broadcast_to(row, (128, BLK)).T
        scale = jnp.concatenate([scale, scale], axis=1)
        out[g, c] = (o[...] * gain[pl.ds(c, 1), :] * scale).astype(bf16)
        out[g, 1 - c] = (r[...].astype(f32) * gain[pl.ds(1 - c, 1), :] * scale).astype(bf16)


def finish(core, gain, parts):
    return pl.pallas_call(
        finish_kernel,
        name="finish",
        in_specs=[SMEM] + [VMEM] * 7,
        out_specs=VMEM,
        out_shape=jax.ShapeDtypeStruct((2, 2, BLK, DH), bf16),
    )(core, gain, *parts[0], *parts[1])


def gather_rows(piece):
    parts = [piece] + [lax.ppermute(piece, "tz", rot(NZ, d)) for d in (1, 2, 3)]
    stack = jnp.stack(parts)
    return [stack] + [lax.ppermute(stack, "tx", rot(NX, d)) for d in (1, 2, 3)]


def scatter_rows(sends):
    own = sends[0]
    recv = [lax.ppermute(sends[d], "tx", rot(NX, d)) for d in (1, 2, 3)]
    y = partial_sum(own, recv)
    return y[0], [lax.ppermute(y[d], "tz", rot(NZ, d)) for d in (1, 2, 3)]


def head_sum(sq):
    sq = sq + sum(lax.ppermute(sq, "hy", rot(4, d)) for d in (1, 2, 3))
    return sq + lax.ppermute(sq, "hz", SWAP)


def pick(array, index, axis):
    return lax.dynamic_index_in_dim(array, index, axis, keepdims=False)


def on_device(
    queries, key_vectors, value_vectors, step_rates, counts, out_gain, w_gate, w_up, w_down
):
    core = lax.axis_index("core").astype(jnp.int32)
    other = 1 - core
    tx = lax.axis_index("tx").astype(jnp.int32)
    tz = lax.axis_index("tz").astype(jnp.int32)
    tok = (tx * NZ + tz) * 2 + core
    tok_other = (tx * NZ + tz) * 2 + other
    grad_scale = float(2 * NX * NZ * BLK) ** (-0.5)

    rows = jnp.concatenate([w_gate, w_up, w_down[:, :, :256], w_down[:, :, 256:]], axis=1)
    own = pick(rows, core, 0)
    recv = lax.ppermute(pick(rows, other, 0), "core", SWAP)
    low = jnp.where(core == 0, own, recv)
    high = jnp.where(core == 0, recv, own)
    masters = jnp.concatenate(
        [low[0:16], high[0:16], low[16:32], high[16:32], low[32:40], high[32:40], low[40:48], high[40:48]]
    )
    piece = masters.astype(bf16)

    limits = counts[:, tok]
    positions = jnp.arange(BLK, dtype=jnp.int32)
    valid = (positions[None, :] < limits[:, None]).astype(f32)
    errors = (
        value_vectors.astype(f32)
        * (step_rates.astype(f32) * grad_scale * valid[:, None, :])[:, :, :, None]
    ).astype(bf16)
    k_own, e_own, q_own = pick(key_vectors, core, 1), pick(errors, core, 1), pick(queries, core, 1)
    k_out, e_out, q_out = pick(key_vectors, other, 1), pick(errors, other, 1), pick(queries, other, 1)
    first = lax.ppermute(jnp.stack([k_out[0], e_out[0]]), "core", SWAP)
    second = lax.ppermute(jnp.stack([k_out[1], e_out[1], q_out[0], q_out[1]]), "core", SWAP)
    k_recv = (first[0], second[0])
    e_recv = (first[1], second[1])
    q_recv = (second[2], second[3])

    stacks = gather_rows(piece)
    parts = []
    for group in range(2):
        pos = jnp.stack([tx, tz, counts[group, tok], counts[group, tok_other]])
        sends = update(pos, stacks, k_own[group], k_recv[group], e_own[group], e_recv[group])
        y0, last = scatter_rows(sends)
        masters, piece = renorm(masters, y0, last)
        stacks = gather_rows(piece)
        o_own, o_send, sq_own, sq_send = apply(pos, stacks, q_own[group], q_recv[group])
        o_recv = lax.ppermute(o_send, "core", SWAP)
        sq = head_sum(sq_own + lax.ppermute(sq_send, "core", SWAP))
        parts.append((o_own, o_recv, sq))
    mixed = finish(core[None], out_gain, parts)

    low = jnp.concatenate([masters[0:16], masters[32:48], masters[64:72], masters[80:88]])
    high = jnp.concatenate([masters[16:32], masters[48:64], masters[72:80], masters[88:96]])
    keep = jnp.where(core == 0, low, high)
    back = lax.ppermute(jnp.where(core == 0, high, low), "core", SWAP)
    final = jnp.stack([jnp.where(core == 0, keep, back), jnp.where(core == 0, back, keep)])
    return (
        mixed,
        final[:, 0:16],
        final[:, 16:32],
        jnp.concatenate([final[:, 32:40], final[:, 40:48]], axis=2),
    )


def solution(mesh):
    grid = Mesh(mesh.devices.reshape(2, 4, NX, NZ, 2), ("hz", "hy", "tx", "tz", "core"))
    head, tok = ("hz", "hy"), ("tx", "tz", "core")
    tokens = P(None, head, tok, None)
    rows = P(head, tok, None)
    return jax.shard_map(
        on_device,
        mesh=grid,
        in_specs=(tokens, tokens, tokens, P(None, head, tok), P(), P(head, None), rows, rows, rows),
        out_specs=(tokens, rows, rows, rows),
        check_vma=False,
    )
```

```python
import functools

import jax
import jax.numpy as jnp
from jax import lax
from jax.experimental import pallas as pl
from jax.experimental.pallas import tpu as pltpu
from jax.sharding import Mesh, PartitionSpec as P

HEADS = 16
DH = 256
FH = 512
BLK = 256
EPS = 1e-06
NX = 4
NZ = 4
ROWS = 96

VMEM = pl.BlockSpec(memory_space=pltpu.VMEM)
SMEM = pl.BlockSpec(memory_space=pltpu.SMEM)
NT = (((1,), (1,)), ((), ()))
NN = (((1,), (0,)), ((), ()))
f32 = jnp.float32
bf16 = jnp.bfloat16


def on_chip(shape, dtype=bf16):
    return pltpu.VMEM(shape, dtype)


def call(kernel, name, operands, outs, scalars=(), hbm=(), scratch=()):
    held = [pltpu.with_memory_space_constraint(v, pltpu.VMEM) for v in operands]
    return pl.pallas_call(
        kernel,
        name=name,
        in_specs=[SMEM] * len(scalars) + [VMEM] * (len(held) + len(hbm)),
        out_specs=[VMEM] * len(outs),
        out_shape=list(outs),
        scratch_shapes=list(scratch),
    )(*scalars, *held, *hbm)


def position():
    return lax.axis_index("tx"), lax.axis_index("tz"), lax.axis_index("core")


def shift(array, axis, d):
    pairs = []
    for i in range(4):
        pairs += [(2 * i, 2 * ((i + d) % 4)), (2 * i + 1, 2 * ((i - d) % 4) + 1)]
    return lax.ppermute(array, (axis, "core"), pairs)


SWAP = [(0, 1), (1, 0)]


def mm(a, b, dims=NN):
    return lax.dot_general(a, b, dims, preferred_element_type=f32)


def chip_index(dx, dz):
    tx, tz, core = position()
    px = lax.rem(tx + jnp.where(core == 0, dx, NX - dx), NX)
    pz = lax.rem(tz + jnp.where(core == 0, dz, NZ - dz), NZ)
    return px * NZ + pz


def assemble(stacks, g_ref, u_ref, d_ref):
    for dx in range(NX):
        for dz in range(NZ):
            p = chip_index((NX - dx) % NX, (NZ - dz) % NZ)
            f0 = pl.multiple_of(p * 32, 32)
            d0 = pl.multiple_of(p * 16, 16)
            g_ref[pl.ds(f0, 32), :] = stacks[dx][dz, 0:32, :]
            u_ref[pl.ds(f0, 32), :] = stacks[dx][dz, 32:64, :]
            d_ref[pl.ds(d0, 16), 0:256] = stacks[dx][dz, 64:80, :]
            d_ref[pl.ds(d0, 16), 256:512] = stacks[dx][dz, 80:96, :]


def split_kernel(wg, wu, wd, own, send):
    core = position()[2]
    for head, out in ((core, own), (1 - core, send)):
        out[0:16, :] = wg[head]
        out[16:32, :] = wu[head]
        out[32:40, :] = wd[head, :, 0:256]
        out[40:48, :] = wd[head, :, 256:512]


def merge_kernel(own, recv, w, piece):
    first = position()[2] == 0
    mine, theirs = own[...], recv[...]
    low = jnp.where(first, mine, theirs)
    high = jnp.where(first, theirs, mine)
    for row, size, to in ((0, 16, 0), (16, 16, 32), (32, 8, 64), (40, 8, 80)):
        w[to : to + size, :] = low[row : row + size]
        w[to + size : to + 2 * size, :] = high[row : row + size]
    piece[...] = w[...].astype(bf16)


def final_kernel(own, recv, wg, wu, wd):
    core = position()[2]
    for head, rows in ((core, own), (1 - core, recv)):
        wg[head] = rows[0:16, :]
        wu[head] = rows[16:32, :]
        wd[head, :, 0:256] = rows[32:40, :]
        wd[head, :, 256:512] = rows[40:48, :]


def tokens_kernel(counts, queries, keys, values, rates, *outs):
    ke_own, q_own, ke_out, q_out = outs[0:2], outs[2:4], outs[4:6], outs[6:8]
    tx, tz, core = position()
    tok = (tx * NZ + tz) * 2 + core
    grad_scale = float(2 * NX * NZ * BLK) ** (-0.5)
    lane = lax.broadcasted_iota(jnp.int32, (1, BLK), 1)
    for head, sends in ((core, False), (1 - core, True)):
        for g in range(2):
            valid = (lane < counts[g, tok]).astype(f32)
            both = rates[g].astype(f32)
            row = jnp.where(head == 0, both[0:1], both[1:2]) * grad_scale * valid
            col = jnp.broadcast_to(row, (128, BLK)).T
            col = jnp.concatenate([col, col], axis=1)
            e = (values[g, head].astype(f32) * col).astype(bf16)
            ke, q = (ke_out[g], q_out[g]) if sends else (ke_own[g], q_own[g])
            ke[0], ke[1], q[...] = keys[g, head], e, queries[g, head]


def update_kernel(
    ke, ke_other, s0, s1, s2, s3, own, o1, o2, o3, g_ref, u_ref, d_ref,
    dt_ref, k_ref, e_ref, et_ref, dg_ref, du_ref, dd_ref,
):
    assemble((s0, s1, s2, s3), g_ref, u_ref, d_ref)
    k_ref[0:BLK, :] = ke[0]
    k_ref[BLK:, :] = ke_other[0]
    e_ref[0:BLK, :] = ke[1]
    e_ref[BLK:, :] = ke_other[1]
    dt_ref[...] = d_ref[...].T
    et_ref[...] = e_ref[...].T
    step = 128

    def chunk(i, carry):
        start = pl.multiple_of(i * step, step)
        rows = pl.ds(start, step)
        a = mm(g_ref[rows, :], k_ref[...], NT)
        b = mm(u_ref[rows, :], k_ref[...], NT)
        r = mm(dt_ref[rows, :], e_ref[...], NT)
        s = jax.nn.sigmoid(a)
        act = a * s
        hid = (act * b).astype(bf16)
        da = (r * b * s * (1.0 + a * (1.0 - s))).astype(bf16)
        db = (r * act).astype(bf16)
        dg_ref[rows, :] = mm(da, k_ref[...])
        du_ref[rows, :] = mm(db, k_ref[...])
        dd_ref[:, rows] = mm(et_ref[...], hid, NT)
        return carry

    for i in range(FH // step):
        chunk(i, 0)
    for dx, out in enumerate((own, o1, o2, o3)):
        for dz in range(NZ):
            p = chip_index(dx, dz)
            f0 = pl.multiple_of(p * 32, 32)
            d0 = pl.multiple_of(p * 16, 16)
            out[dz, 0:32, :] = dg_ref[pl.ds(f0, 32), :].astype(out.dtype)
            out[dz, 32:64, :] = du_ref[pl.ds(f0, 32), :].astype(out.dtype)
            out[dz, 64:80, :] = dd_ref[pl.ds(d0, 16), 0:256].astype(out.dtype)
            out[dz, 80:96, :] = dd_ref[pl.ds(d0, 16), 256:512].astype(out.dtype)


WEIGHTS = (((FH, DH), bf16), ((FH, DH), bf16), ((DH, FH), bf16))


def update(stacks, ke, ke_other, keep):
    weights = [on_chip(*w) for w in WEIGHTS]
    outs = [on_chip((NZ, ROWS, DH), f32)] + [on_chip((NZ, ROWS, DH))] * 3
    scratch = [
        pltpu.VMEM((FH, DH), bf16),
        pltpu.VMEM((2 * BLK, DH), bf16),
        pltpu.VMEM((2 * BLK, DH), bf16),
        pltpu.VMEM((DH, 2 * BLK), bf16),
        pltpu.VMEM((FH, DH), f32),
        pltpu.VMEM((FH, DH), f32),
        pltpu.VMEM((DH, FH), f32),
    ]
    operands = (ke, ke_other, *stacks)
    if keep:
        got = call(update_kernel, "update", operands, outs + weights, scratch=scratch)
        return got[:4], got[4:]
    return call(update_kernel, "update", operands, outs, scratch=weights + scratch), None


def partial_kernel(own, r1, r2, r3, y0, y1, y2, y3):
    for dz, out in enumerate((y0, y1, y2, y3)):
        total = own[dz] + r1[dz].astype(f32) + r2[dz].astype(f32) + r3[dz].astype(f32)
        out[...] = total.astype(out.dtype)


def partial_sum(own, recv):
    return call(
        partial_kernel,
        "partial_sum",
        (own, *recv),
        [on_chip((ROWS, DH), f32)] + [on_chip((ROWS, DH))] * 3,
    )


def renorm_kernel(w, y0, t1, t2, t3, piece, *outs, last):
    old = w[...]
    new = old + (y0[...] + t1[...].astype(f32) + t2[...].astype(f32) + t3[...].astype(f32))

    def mean_square(v):
        sums = jnp.sum(v * v, axis=-1, keepdims=True)
        wide = (sums[64:80] + sums[80:96]) * (1.0 / FH)
        return jnp.concatenate([sums[0:64] * (1.0 / DH), wide, wide], axis=0)

    scaled = new * jnp.sqrt(mean_square(old)) * lax.rsqrt(mean_square(new) + EPS)
    piece[...] = scaled.astype(bf16)
    if not last:
        outs[0][...] = scaled
        return
    first = position()[2] == 0
    for row, size, at in ((0, 16, 0), (16, 16, 32), (32, 8, 64), (40, 8, 80)):
        low = scaled[at : at + size, :]
        high = scaled[at + size : at + 2 * size, :]
        outs[0][row : row + size, :] = jnp.where(first, low, high)
        outs[1][row : row + size, :] = jnp.where(first, high, low)


def renorm(w, y0, recv, last=False):
    held = [on_chip((48, DH), f32)] * 2 if last else [on_chip((ROWS, DH), f32)]
    return call(
        functools.partial(renorm_kernel, last=last),
        "renorm",
        (w, y0, *recv),
        [on_chip((ROWS, DH)), *held],
    )


def apply_kernel(counts, q, q_other, *refs, group, assembled):
    if assembled:
        g_ref, u_ref, d_ref, o_own, o_send, sq = refs
    else:
        o_own, o_send, sq, g_ref, u_ref, d_ref = refs[4:]
        assemble(refs[:4], g_ref, u_ref, d_ref)
    tx, tz, core = position()
    tok = (tx * NZ + tz) * 2
    for which, (query, out, dev) in enumerate(
        ((q, o_own, tok + core), (q_other, o_send, tok + 1 - core))
    ):
        a = mm(query[...], g_ref[...], NT)
        b = mm(query[...], u_ref[...], NT)
        hid = (a * jax.nn.sigmoid(a) * b).astype(bf16)
        o = mm(hid, d_ref[...], NT)
        valid = lax.broadcasted_iota(jnp.int32, (BLK, DH), 0) < counts[group, dev]
        o = jnp.where(valid, o, 0.0)
        out[...] = o.astype(out.dtype)
        sums = jnp.sum(o * o, axis=-1, keepdims=True)
        sq[which] = jnp.broadcast_to(sums, (BLK, 128)).T[0:4, :]


def apply(counts, q, q_other, weights, group, assembled):
    return call(
        functools.partial(apply_kernel, group=group, assembled=assembled),
        "apply",
        (q, q_other, *weights),
        [on_chip((BLK, DH), f32), on_chip((BLK, DH)), on_chip((2, 4, BLK), f32)],
        scalars=(counts,),
        scratch=() if assembled else [pltpu.VMEM(*w) for w in WEIGHTS],
    )


def finish_kernel(o0, r0, o1, r1, sq, gain, out):
    core = position()[2]
    for g, (o, r) in enumerate(((o0, r0), (o1, r1))):
        row = lax.rsqrt(sq[4 * g : 4 * g + 1, :] * (1.0 / (HEADS * DH)) + EPS)
        scale = jnp.broadcast_to(row, (128, BLK)).T
        scale = jnp.concatenate([scale, scale], axis=1)
        out[g, core] = (o[...] * gain[pl.ds(core, 1), :] * scale).astype(bf16)
        out[g, 1 - core] = (r[...].astype(f32) * gain[pl.ds(1 - core, 1), :] * scale).astype(bf16)


def gather_rows(piece):
    parts = [piece] + [shift(piece, "tz", d) for d in (1, 2, 3)]
    stack = jnp.stack(parts)
    return [stack] + [shift(stack, "tx", d) for d in (1, 2, 3)]


def scatter_rows(sends):
    recv = [shift(sends[d], "tx", d) for d in (1, 2, 3)]
    y = partial_sum(sends[0], recv)
    return y[0], [shift(y[d], "tz", d) for d in (1, 2, 3)]


def head_sum(sq):
    sq = sq + sum(shift(sq, "hy", d) for d in (1, 2, 3))
    return sq + lax.ppermute(sq, "hz", SWAP)


def swap(array):
    return lax.ppermute(array, "core", SWAP)


def on_device(
    queries, key_vectors, value_vectors, step_rates, counts, out_gain, w_gate, w_up, w_down
):
    half = on_chip((48, DH), f32)
    own, send = call(split_kernel, "split", (), [half, half], hbm=(w_gate, w_up, w_down))
    masters, piece = call(
        merge_kernel, "merge", (own, swap(send)), [on_chip((ROWS, DH), f32), on_chip((ROWS, DH))]
    )
    piece, tokens = lax.optimization_barrier(
        (piece, (queries, key_vectors, value_vectors, step_rates))
    )
    pair, single = on_chip((2, BLK, DH)), on_chip((BLK, DH))
    got = call(
        tokens_kernel,
        "tokens",
        (),
        [pair, pair, single, single] * 2,
        scalars=(counts,),
        hbm=tokens,
    )
    ke, q = got[0:2], got[2:4]
    ke_other, q_other = [swap(v) for v in got[4:6]], [swap(v) for v in got[6:8]]

    stacks = gather_rows(piece)
    sends, _ = update(stacks, ke[0], ke_other[0], False)
    piece, masters = renorm(masters, *scatter_rows(sends))
    stacks = gather_rows(piece)
    sends, weights = update(stacks, ke[1], ke_other[1], True)
    o0, o0_send, sq0 = apply(counts, q[0], q_other[0], weights, 0, True)
    r0 = swap(o0_send)
    piece, own, send = renorm(masters, *scatter_rows(sends), last=True)
    stacks = gather_rows(piece)
    held = [pltpu.with_memory_space_constraint(v, pltpu.VMEM) for v in (own, swap(send))]
    finals = pl.pallas_call(
        final_kernel,
        name="final",
        in_specs=[VMEM] * 2,
        out_specs=[VMEM] * 3,
        out_shape=[
            jax.ShapeDtypeStruct((2, 16, DH), f32),
            jax.ShapeDtypeStruct((2, 16, DH), f32),
            jax.ShapeDtypeStruct((2, 8, FH), f32),
        ],
    )(*held)
    stacks[0], finals = lax.optimization_barrier((stacks[0], finals))
    o1, o1_send, sq1 = apply(counts, q[1], q_other[1], stacks, 1, False)
    sq = jnp.concatenate([sq0, sq1], axis=1)
    total = head_sum(sq[0] + swap(sq[1]))
    r1 = swap(o1_send)
    held = [pltpu.with_memory_space_constraint(v, pltpu.VMEM) for v in (o0, r0, o1, r1, total)]
    mixed = pl.pallas_call(
        finish_kernel,
        name="finish",
        in_specs=[VMEM] * 6,
        out_specs=VMEM,
        out_shape=jax.ShapeDtypeStruct((2, 2, BLK, DH), bf16),
    )(*held, out_gain)
    return (mixed, *finals)


def solution(mesh):
    grid = Mesh(mesh.devices.reshape(2, 4, NX, NZ, 2), ("hz", "hy", "tx", "tz", "core"))
    head, tok = ("hz", "hy"), ("tx", "tz", "core")
    tokens = P(None, head, tok, None)
    rows = P(head, tok, None)
    return jax.shard_map(
        on_device,
        mesh=grid,
        in_specs=(tokens, tokens, tokens, P(None, head, tok), P(), P(head, None), rows, rows, rows),
        out_specs=(tokens, rows, rows, rows),
        check_vma=False,
    )
```

```python
import functools

import jax
import jax.numpy as jnp
from jax import lax
from jax.experimental import pallas as pl
from jax.experimental.pallas import tpu as pltpu
from jax.sharding import Mesh, PartitionSpec as P

HEADS = 16
DH = 256
FH = 512
BLK = 256
EPS = 1e-06
NX = 4
NZ = 4
ROWS = 96

VMEM = pl.BlockSpec(memory_space=pltpu.VMEM)
SMEM = pl.BlockSpec(memory_space=pltpu.SMEM)
NT = (((1,), (1,)), ((), ()))
NN = (((1,), (0,)), ((), ()))
f32 = jnp.float32
bf16 = jnp.bfloat16


def on_chip(shape, dtype=bf16):
    return pltpu.VMEM(shape, dtype)


def call(kernel, operands, outs, scalars=(), hbm=(), scratch=(), limit=8):
    held = [pltpu.with_memory_space_constraint(v, pltpu.VMEM) for v in operands]
    hbm = [pltpu.with_memory_space_constraint(v, pltpu.HBM) for v in hbm]
    return pl.pallas_call(
        kernel,
        in_specs=[SMEM] * len(scalars) + [VMEM] * (len(held) + len(hbm)),
        out_specs=[VMEM] * len(outs),
        out_shape=list(outs),
        scratch_shapes=list(scratch),
        compiler_params=pltpu.CompilerParams(vmem_limit_bytes=limit << 20),
    )(*scalars, *held, *hbm)


def position():
    return lax.axis_index("tx"), lax.axis_index("tz"), lax.axis_index("core")


def shift(array, axis, d):
    pairs = []
    for i in range(4):
        pairs += [(2 * i, 2 * (i ^ d)), (2 * i + 1, 2 * (i ^ ((4 - d) % 4)) + 1)]
    return lax.ppermute(array, (axis, "core"), pairs)


SWAP = [(0, 1), (1, 0)]


def mm(a, b, dims=NN):
    return lax.dot_general(a, b, dims, preferred_element_type=f32)


def chip_index(dx, dz):
    tx, tz, core = position()
    px = jnp.bitwise_xor(tx, jnp.where(core == 0, dx, (4 - dx) % 4))
    pz = jnp.bitwise_xor(tz, jnp.where(core == 0, dz, (4 - dz) % 4))
    return px * NZ + pz


def assemble(stacks, g_ref, u_ref, d_ref):
    for dx in range(NX):
        for dz in range(NZ):
            p = chip_index(dx, dz)
            f0 = pl.multiple_of(p * 32, 32)
            d0 = pl.multiple_of(p * 16, 16)
            g_ref[pl.ds(f0, 32), :] = stacks[dx][dz, 0:32, :]
            u_ref[pl.ds(f0, 32), :] = stacks[dx][dz, 32:64, :]
            d_ref[pl.ds(d0, 16), 0:256] = stacks[dx][dz, 64:80, :]
            d_ref[pl.ds(d0, 16), 256:512] = stacks[dx][dz, 80:96, :]


def split_kernel(wg, wu, wd, own, send):
    core = position()[2]
    for head, out in ((core, own), (1 - core, send)):
        out[0:16, :] = wg[head]
        out[16:32, :] = wu[head]
        out[32:40, :] = wd[head, :, 0:256]
        out[40:48, :] = wd[head, :, 256:512]


def merge_kernel(own, recv, w, piece):
    first = position()[2] == 0
    mine, theirs = own[...], recv[...]
    low = jnp.where(first, mine, theirs)
    high = jnp.where(first, theirs, mine)
    for row, size, to in ((0, 16, 0), (16, 16, 32), (32, 8, 64), (40, 8, 80)):
        w[to : to + size, :] = low[row : row + size]
        w[to + size : to + 2 * size, :] = high[row : row + size]
    piece[...] = w[...].astype(bf16)


def final_kernel(own, recv, wg, wu, wd):
    core = position()[2]
    for head, rows in ((core, own), (1 - core, recv)):
        wg[head] = rows[0:16, :]
        wu[head] = rows[16:32, :]
        wd[head, :, 0:256] = rows[32:40, :]
        wd[head, :, 256:512] = rows[40:48, :]


def tokens_kernel(counts, queries, keys, values, rates, gain_in, *outs):
    outs[8][...] = gain_in[...]
    ke_own, q_own, ke_out, q_out = outs[0:2], outs[2:4], outs[4:6], outs[6:8]
    tx, tz, core = position()
    tok = (tx * NZ + tz) * 2 + core
    grad_scale = float(2 * NX * NZ * BLK) ** (-0.5)
    lane = lax.broadcasted_iota(jnp.int32, (1, BLK), 1)
    for head, sends in ((core, False), (1 - core, True)):
        for g in range(2):
            valid = (lane < counts[g, tok]).astype(f32)
            both = rates[g].astype(f32)
            row = jnp.where(head == 0, both[0:1], both[1:2]) * grad_scale * valid
            col = jnp.broadcast_to(row, (128, BLK)).T
            col = jnp.concatenate([col, col], axis=1)
            e = (values[g, head].astype(f32) * col).astype(bf16)
            ke, q = (ke_out[g], q_out[g]) if sends else (ke_own[g], q_own[g])
            ke[0], ke[1], q[...] = keys[g, head], e, queries[g, head]


def update_kernel(
    ke, ke_other, s0, s1, s2, s3, own, o1, o2, o3, g_ref, u_ref, d_ref,
    dt_ref, k_ref, e_ref, et_ref, dg_ref, du_ref, dd_ref,
):
    assemble((s0, s1, s2, s3), g_ref, u_ref, d_ref)
    k_ref[0:BLK, :] = ke[0]
    k_ref[BLK:, :] = ke_other[0]
    e_ref[0:BLK, :] = ke[1]
    e_ref[BLK:, :] = ke_other[1]
    dt_ref[...] = d_ref[...].T
    et_ref[...] = e_ref[...].T
    a = mm(g_ref[...], k_ref[...], NT)
    b = mm(u_ref[...], k_ref[...], NT)
    r = mm(dt_ref[...], e_ref[...], NT)
    s = jax.nn.sigmoid(a)
    act = a * s
    hid = (act * b).astype(bf16)
    da = (r * b * s * (1.0 + a * (1.0 - s))).astype(bf16)
    db = (r * act).astype(bf16)
    dg_ref[...] = mm(da, k_ref[...])
    du_ref[...] = mm(db, k_ref[...])
    dd_ref[...] = mm(et_ref[...], hid, NT)
    for dx, out in enumerate((own, o1, o2, o3)):
        for dz in range(NZ):
            p = chip_index(dx, dz)
            f0 = pl.multiple_of(p * 32, 32)
            d0 = pl.multiple_of(p * 16, 16)
            out[dz, 0:32, :] = dg_ref[pl.ds(f0, 32), :].astype(out.dtype)
            out[dz, 32:64, :] = du_ref[pl.ds(f0, 32), :].astype(out.dtype)
            out[dz, 64:80, :] = dd_ref[pl.ds(d0, 16), 0:256].astype(out.dtype)
            out[dz, 80:96, :] = dd_ref[pl.ds(d0, 16), 256:512].astype(out.dtype)


WEIGHTS = (((FH, DH), bf16), ((FH, DH), bf16), ((DH, FH), bf16))


def update(stacks, ke, ke_other, keep):
    weights = [on_chip(*w) for w in WEIGHTS]
    outs = [on_chip((NZ, ROWS, DH), f32)] + [on_chip((NZ, ROWS, DH))] * 3
    scratch = [
        pltpu.VMEM((FH, DH), bf16),
        pltpu.VMEM((2 * BLK, DH), bf16),
        pltpu.VMEM((2 * BLK, DH), bf16),
        pltpu.VMEM((DH, 2 * BLK), bf16),
        pltpu.VMEM((FH, DH), f32),
        pltpu.VMEM((FH, DH), f32),
        pltpu.VMEM((DH, FH), f32),
    ]
    operands = (ke, ke_other, *stacks)
    if keep:
        got = call(update_kernel, operands, outs + weights, scratch=scratch, limit=20)
        return got[:4], got[4:]
    return call(update_kernel, operands, outs, scratch=weights + scratch, limit=20), None


def partial_kernel(own, r1, r2, r3, y0, y1, y2, y3):
    for dz, out in enumerate((y0, y1, y2, y3)):
        total = own[dz] + r1[dz].astype(f32) + r2[dz].astype(f32) + r3[dz].astype(f32)
        out[...] = total.astype(out.dtype)


def partial_sum(own, recv):
    return call(
        partial_kernel, (own, *recv), [on_chip((ROWS, DH), f32)] + [on_chip((ROWS, DH))] * 3
    )


def renorm_kernel(w, y0, t1, t2, t3, piece, *outs, last):
    old = w[...]
    new = old + (y0[...] + t1[...].astype(f32) + t2[...].astype(f32) + t3[...].astype(f32))

    def mean_square(v):
        sums = jnp.sum(v * v, axis=-1, keepdims=True)
        wide = (sums[64:80] + sums[80:96]) * (1.0 / FH)
        return jnp.concatenate([sums[0:64] * (1.0 / DH), wide, wide], axis=0)

    scaled = new * jnp.sqrt(mean_square(old)) * lax.rsqrt(mean_square(new) + EPS)
    piece[...] = scaled.astype(bf16)
    if not last:
        outs[0][...] = scaled
        return
    first = position()[2] == 0
    for row, size, at in ((0, 16, 0), (16, 16, 32), (32, 8, 64), (40, 8, 80)):
        low = scaled[at : at + size, :]
        high = scaled[at + size : at + 2 * size, :]
        outs[0][row : row + size, :] = jnp.where(first, low, high)
        outs[1][row : row + size, :] = jnp.where(first, high, low)


def renorm(w, y0, recv, last=False):
    held = [on_chip((48, DH), f32)] * 2 if last else [on_chip((ROWS, DH), f32)]
    return call(
        functools.partial(renorm_kernel, last=last), (w, y0, *recv), [on_chip((ROWS, DH)), *held]
    )


def apply_kernel(q, q_other, *refs, assembled):
    if assembled:
        g_ref, u_ref, d_ref, o_own, o_send, sq = refs
    else:
        o_own, o_send, sq, g_ref, u_ref, d_ref = refs[4:]
        assemble(refs[:4], g_ref, u_ref, d_ref)
    for which, (query, out) in enumerate(((q, o_own), (q_other, o_send))):
        a = mm(query[...], g_ref[...], NT)
        b = mm(query[...], u_ref[...], NT)
        hid = (a * jax.nn.sigmoid(a) * b).astype(bf16)
        o = mm(hid, d_ref[...], NT)
        out[...] = o.astype(out.dtype)
        sums = jnp.sum(o * o, axis=-1, keepdims=True)
        sq[which] = jnp.broadcast_to(sums, (BLK, 128)).T[0:4, :]


def apply(q, q_other, weights, assembled):
    return call(
        functools.partial(apply_kernel, assembled=assembled),
        (q, q_other, *weights),
        [on_chip((BLK, DH), f32), on_chip((BLK, DH)), on_chip((2, 4, BLK), f32)],
        scratch=() if assembled else [pltpu.VMEM(*w) for w in WEIGHTS],
        limit=16,
    )


def finish_kernel(counts, o0, r0, o1, r1, sq, gain, out):
    tx, tz, core = position()
    tok = (tx * NZ + tz) * 2 + core
    for g, (own, other) in enumerate(((o0, r0), (o1, r1))):
        valid = lax.broadcasted_iota(jnp.int32, (1, BLK), 1) < counts[g, tok]
        row = lax.rsqrt(sq[4 * g : 4 * g + 1, :] * (1.0 / (HEADS * DH)) + EPS)
        scale = jnp.broadcast_to(jnp.where(valid, row, 0.0), (128, BLK)).T
        scale = jnp.concatenate([scale, scale], axis=1)
        for head, o in ((core, own), (1 - core, other)):
            out[g, head] = (o[...].astype(f32) * gain[pl.ds(head, 1), :] * scale).astype(bf16)


def gather_rows(piece):
    parts = [piece] + [shift(piece, "tz", d) for d in (1, 2, 3)]
    stack = jnp.stack(parts)
    return [stack] + [shift(stack, "tx", d) for d in (1, 2, 3)]


def scatter_rows(sends):
    recv = [shift(sends[d], "tx", d) for d in (1, 2, 3)]
    y = partial_sum(sends[0], recv)
    return y[0], [shift(y[d], "tz", d) for d in (1, 2, 3)]


def head_sum(sq):
    sq = sq + sum(shift(sq, "hy", d) for d in (1, 2, 3))
    return sq + lax.ppermute(sq, "hz", SWAP)


def swap(array):
    return lax.ppermute(array, "core", SWAP)


def on_device(
    queries, key_vectors, value_vectors, step_rates, counts, out_gain, w_gate, w_up, w_down
):
    half = on_chip((48, DH), f32)
    own, send = call(split_kernel, (), [half, half], hbm=(w_gate, w_up, w_down))
    masters, piece = call(
        merge_kernel, (own, swap(send)), [on_chip((ROWS, DH), f32), on_chip((ROWS, DH))]
    )
    piece, tokens = lax.optimization_barrier(
        (piece, (queries, key_vectors, value_vectors, step_rates))
    )
    pair, single = on_chip((2, BLK, DH)), on_chip((BLK, DH))
    got = call(
        tokens_kernel,
        (),
        [pair, pair, single, single] * 2 + [on_chip((2, DH), f32)],
        scalars=(counts,),
        hbm=(*tokens, out_gain),
        limit=16,
    )
    ke, q = got[0:2], got[2:4]
    ke_other = [swap(v) for v in got[4:6]]
    q_other = [swap(v) for v in got[6:8]]

    stacks = gather_rows(piece)
    sends, _ = update(stacks, ke[0], ke_other[0], False)
    piece, masters = renorm(masters, *scatter_rows(sends))
    stacks = gather_rows(piece)
    sends, weights = update(stacks, ke[1], ke_other[1], True)
    o0, o0_send, sq0 = apply(q[0], q_other[0], weights, True)
    r0 = swap(o0_send)
    piece, own, send = renorm(masters, *scatter_rows(sends), last=True)
    stacks = gather_rows(piece)
    finals = call(
        final_kernel,
        (own, swap(send)),
        [
            jax.ShapeDtypeStruct((2, 16, DH), f32),
            jax.ShapeDtypeStruct((2, 16, DH), f32),
            jax.ShapeDtypeStruct((2, 8, FH), f32),
        ],
    )
    stacks[0], finals = lax.optimization_barrier((stacks[0], finals))
    o1, o1_send, sq1 = apply(q[1], q_other[1], stacks, False)
    sq = jnp.concatenate([sq0, sq1], axis=1)
    total = head_sum(sq[0] + swap(sq[1]))
    r1 = swap(o1_send)
    (mixed,) = call(
        finish_kernel,
        (o0, r0, o1, r1, total, got[8]),
        [jax.ShapeDtypeStruct((2, 2, BLK, DH), bf16)],
        scalars=(counts,),
    )
    return (mixed, *finals)


def solution(mesh):
    grid = Mesh(mesh.devices.reshape(2, 4, NX, NZ, 2), ("hz", "hy", "tx", "tz", "core"))
    head, tok = ("hz", "hy"), ("tx", "tz", "core")
    tokens = P(None, head, tok, None)
    rows = P(head, tok, None)
    return jax.shard_map(
        on_device,
        mesh=grid,
        in_specs=(tokens, tokens, tokens, P(None, head, tok), P(), P(head, None), rows, rows, rows),
        out_specs=(tokens, rows, rows, rows),
        check_vma=False,
    )
```

```python
import functools

import jax
import jax.numpy as jnp
from jax import lax
from jax.experimental import pallas as pl
from jax.experimental.pallas import tpu as pltpu
from jax.sharding import Mesh, PartitionSpec as P

HEADS = 16
DH = 256
FH = 512
BLK = 256
EPS = 1e-06
NX = 4
NZ = 4
ROWS = 96

VMEM = pl.BlockSpec(memory_space=pltpu.VMEM)
SMEM = pl.BlockSpec(memory_space=pltpu.SMEM)
NT = (((1,), (1,)), ((), ()))
NN = (((1,), (0,)), ((), ()))
f32 = jnp.float32
bf16 = jnp.bfloat16


def on_chip(shape, dtype=bf16):
    return pltpu.VMEM(shape, dtype)


def call(kernel, operands, outs, scalars=(), hbm=(), scratch=(), limit=8):
    held = [pltpu.with_memory_space_constraint(v, pltpu.VMEM) for v in operands]
    hbm = [pltpu.with_memory_space_constraint(v, pltpu.HBM) for v in hbm]
    return pl.pallas_call(
        kernel,
        in_specs=[SMEM] * len(scalars) + [VMEM] * (len(held) + len(hbm)),
        out_specs=[VMEM] * len(outs),
        out_shape=list(outs),
        scratch_shapes=list(scratch),
        compiler_params=pltpu.CompilerParams(vmem_limit_bytes=limit << 20),
    )(*scalars, *held, *hbm)


def position():
    return lax.axis_index("tx"), lax.axis_index("tz"), lax.axis_index("core")


def shift(array, axis, d):
    pairs = []
    for i in range(4):
        pairs += [(2 * i, 2 * (i ^ d)), (2 * i + 1, 2 * (i ^ ((4 - d) % 4)) + 1)]
    return lax.ppermute(array, (axis, "core"), pairs)


SWAP = [(0, 1), (1, 0)]


def mm(a, b, dims=NN):
    return lax.dot_general(a, b, dims, preferred_element_type=f32)


def chip_index(dx, dz):
    tx, tz, core = position()
    px = jnp.bitwise_xor(tx, jnp.where(core == 0, dx, (4 - dx) % 4))
    pz = jnp.bitwise_xor(tz, jnp.where(core == 0, dz, (4 - dz) % 4))
    return px * NZ + pz


def assemble(stacks, g_ref, u_ref, d_ref):
    for dx in range(NX):
        for dz in range(NZ):
            p = chip_index(dx, dz)
            f0 = pl.multiple_of(p * 32, 32)
            d0 = pl.multiple_of(p * 16, 16)
            g_ref[pl.ds(f0, 32), :] = stacks[dx][dz, 0:32, :]
            u_ref[pl.ds(f0, 32), :] = stacks[dx][dz, 32:64, :]
            d_ref[pl.ds(d0, 16), 0:256] = stacks[dx][dz, 64:80, :]
            d_ref[pl.ds(d0, 16), 256:512] = stacks[dx][dz, 80:96, :]


def split_kernel(wg, wu, wd, own, send):
    core = position()[2]
    for head, out in ((core, own), (1 - core, send)):
        out[0:16, :] = wg[head]
        out[16:32, :] = wu[head]
        out[32:40, :] = wd[head, :, 0:256]
        out[40:48, :] = wd[head, :, 256:512]


def merge_kernel(own, recv, w, piece):
    first = position()[2] == 0
    mine, theirs = own[...], recv[...]
    low = jnp.where(first, mine, theirs)
    high = jnp.where(first, theirs, mine)
    for row, size, to in ((0, 16, 0), (16, 16, 32), (32, 8, 64), (40, 8, 80)):
        w[to : to + size, :] = low[row : row + size]
        w[to + size : to + 2 * size, :] = high[row : row + size]
    piece[...] = w[...].astype(bf16)


def final_kernel(own, recv, wg, wu, wd):
    core = position()[2]
    for head, rows in ((core, own), (1 - core, recv)):
        wg[head] = rows[0:16, :]
        wu[head] = rows[16:32, :]
        wd[head, :, 0:256] = rows[32:40, :]
        wd[head, :, 256:512] = rows[40:48, :]


def tokens_kernel(counts, queries, keys, values, rates, gain_in, *outs):
    outs[8][...] = gain_in[...]
    masks = outs[9]
    ke_own, q_own, ke_out, q_out = outs[0:2], outs[2:4], outs[4:6], outs[6:8]
    tx, tz, core = position()
    tok = (tx * NZ + tz) * 2 + core
    grad_scale = float(2 * NX * NZ * BLK) ** (-0.5)
    lane = lax.broadcasted_iota(jnp.int32, (1, BLK), 1)
    for head, sends in ((core, False), (1 - core, True)):
        for g in range(2):
            valid = (lane < counts[g, tok]).astype(f32)
            masks[g : g + 1, :] = valid
            both = rates[g].astype(f32)
            row = jnp.where(head == 0, both[0:1], both[1:2]) * grad_scale * valid
            col = jnp.broadcast_to(row, (128, BLK)).T
            col = jnp.concatenate([col, col], axis=1)
            e = (values[g, head].astype(f32) * col).astype(bf16)
            ke, q = (ke_out[g], q_out[g]) if sends else (ke_own[g], q_own[g])
            ke[0], ke[1], q[...] = keys[g, head], e, queries[g, head]


def update_kernel(
    ke, ke_other, s0, s1, s2, s3, own, o1, o2, o3, g_ref, u_ref, d_ref,
    dt_ref, k_ref, e_ref, et_ref, dg_ref, du_ref, dd_ref,
):
    assemble((s0, s1, s2, s3), g_ref, u_ref, d_ref)
    k_ref[0:BLK, :] = ke[0]
    k_ref[BLK:, :] = ke_other[0]
    e_ref[0:BLK, :] = ke[1]
    e_ref[BLK:, :] = ke_other[1]
    dt_ref[...] = d_ref[...].T
    et_ref[...] = e_ref[...].T
    a = mm(g_ref[...], k_ref[...], NT)
    b = mm(u_ref[...], k_ref[...], NT)
    r = mm(dt_ref[...], e_ref[...], NT)
    s = jax.nn.sigmoid(a)
    act = a * s
    hid = (act * b).astype(bf16)
    da = (r * b * s * (1.0 + a * (1.0 - s))).astype(bf16)
    db = (r * act).astype(bf16)
    dg_ref[...] = mm(da, k_ref[...])
    du_ref[...] = mm(db, k_ref[...])
    dd_ref[...] = mm(et_ref[...], hid, NT)
    for dx, out in enumerate((own, o1, o2, o3)):
        for dz in range(NZ):
            p = chip_index(dx, dz)
            f0 = pl.multiple_of(p * 32, 32)
            d0 = pl.multiple_of(p * 16, 16)
            out[dz, 0:32, :] = dg_ref[pl.ds(f0, 32), :].astype(out.dtype)
            out[dz, 32:64, :] = du_ref[pl.ds(f0, 32), :].astype(out.dtype)
            out[dz, 64:80, :] = dd_ref[pl.ds(d0, 16), 0:256].astype(out.dtype)
            out[dz, 80:96, :] = dd_ref[pl.ds(d0, 16), 256:512].astype(out.dtype)


WEIGHTS = (((FH, DH), bf16), ((FH, DH), bf16), ((DH, FH), bf16))


def update(stacks, ke, ke_other, keep):
    weights = [on_chip(*w) for w in WEIGHTS]
    outs = [on_chip((NZ, ROWS, DH), f32)] + [on_chip((NZ, ROWS, DH))] * 3
    scratch = [
        pltpu.VMEM((FH, DH), bf16),
        pltpu.VMEM((2 * BLK, DH), bf16),
        pltpu.VMEM((2 * BLK, DH), bf16),
        pltpu.VMEM((DH, 2 * BLK), bf16),
        pltpu.VMEM((FH, DH), f32),
        pltpu.VMEM((FH, DH), f32),
        pltpu.VMEM((DH, FH), f32),
    ]
    operands = (ke, ke_other, *stacks)
    if keep:
        got = call(update_kernel, operands, outs + weights, scratch=scratch, limit=20)
        return got[:4], got[4:]
    return call(update_kernel, operands, outs, scratch=weights + scratch, limit=20), None


def partial_kernel(own, r1, r2, r3, y0, y1, y2, y3):
    for dz, out in enumerate((y0, y1, y2, y3)):
        total = own[dz] + r1[dz].astype(f32) + r2[dz].astype(f32) + r3[dz].astype(f32)
        out[...] = total.astype(out.dtype)


def partial_sum(own, recv):
    return call(
        partial_kernel, (own, *recv), [on_chip((ROWS, DH), f32)] + [on_chip((ROWS, DH))] * 3
    )


def renorm_kernel(w, y0, t1, t2, t3, piece, *outs, last):
    old = w[...]
    new = old + (y0[...] + t1[...].astype(f32) + t2[...].astype(f32) + t3[...].astype(f32))

    def mean_square(v):
        sums = jnp.sum(v * v, axis=-1, keepdims=True)
        wide = (sums[64:80] + sums[80:96]) * (1.0 / FH)
        return jnp.concatenate([sums[0:64] * (1.0 / DH), wide, wide], axis=0)

    scaled = new * jnp.sqrt(mean_square(old)) * lax.rsqrt(mean_square(new) + EPS)
    piece[...] = scaled.astype(bf16)
    if not last:
        outs[0][...] = scaled
        return
    first = position()[2] == 0
    for row, size, at in ((0, 16, 0), (16, 16, 32), (32, 8, 64), (40, 8, 80)):
        low = scaled[at : at + size, :]
        high = scaled[at + size : at + 2 * size, :]
        outs[0][row : row + size, :] = jnp.where(first, low, high)
        outs[1][row : row + size, :] = jnp.where(first, high, low)


def renorm(w, y0, recv, last=False):
    held = [on_chip((48, DH), f32)] * 2 if last else [on_chip((ROWS, DH), f32)]
    return call(
        functools.partial(renorm_kernel, last=last), (w, y0, *recv), [on_chip((ROWS, DH)), *held]
    )


def apply_kernel(q, q_other, *refs, assembled):
    if assembled:
        g_ref, u_ref, d_ref, o_own, o_send, sq = refs
    else:
        o_own, o_send, sq, g_ref, u_ref, d_ref = refs[4:]
        assemble(refs[:4], g_ref, u_ref, d_ref)
    for which, (query, out) in enumerate(((q, o_own), (q_other, o_send))):
        a = mm(query[...], g_ref[...], NT)
        b = mm(query[...], u_ref[...], NT)
        hid = (a * jax.nn.sigmoid(a) * b).astype(bf16)
        o = mm(hid, d_ref[...], NT)
        out[...] = o.astype(out.dtype)
        sums = jnp.sum(o * o, axis=-1, keepdims=True)
        sq[which] = jnp.broadcast_to(sums, (BLK, 128)).T[0:4, :]


def apply(q, q_other, weights, assembled):
    return call(
        functools.partial(apply_kernel, assembled=assembled),
        (q, q_other, *weights),
        [on_chip((BLK, DH), f32), on_chip((BLK, DH)), on_chip((2, 4, BLK), f32)],
        scratch=() if assembled else [pltpu.VMEM(*w) for w in WEIGHTS],
        limit=16,
    )


def finish_kernel(o0, r0, o1, r1, sq, gain, masks, out):
    core = position()[2]
    for g, (own, other) in enumerate(((o0, r0), (o1, r1))):
        row = lax.rsqrt(sq[4 * g : 4 * g + 1, :] * (1.0 / (HEADS * DH)) + EPS)
        scale = jnp.broadcast_to(row * masks[g : g + 1, :], (128, BLK)).T
        scale = jnp.concatenate([scale, scale], axis=1)
        for head, o in ((core, own), (1 - core, other)):
            out[g, head] = (o[...].astype(f32) * gain[pl.ds(head, 1), :] * scale).astype(bf16)


def gather_rows(piece):
    parts = [piece] + [shift(piece, "tz", d) for d in (1, 2, 3)]
    stack = jnp.stack(parts)
    return [stack] + [shift(stack, "tx", d) for d in (1, 2, 3)]


def scatter_rows(sends):
    recv = [shift(sends[d], "tx", d) for d in (1, 2, 3)]
    y = partial_sum(sends[0], recv)
    return y[0], [shift(y[d], "tz", d) for d in (1, 2, 3)]


def head_sum(sq):
    sq = sq + sum(shift(sq, "hy", d) for d in (1, 2, 3))
    return sq + lax.ppermute(sq, "hz", SWAP)


def swap(array):
    return lax.ppermute(array, "core", SWAP)


def on_device(
    queries, key_vectors, value_vectors, step_rates, counts, out_gain, w_gate, w_up, w_down
):
    half = on_chip((48, DH), f32)
    own, send = call(split_kernel, (), [half, half], hbm=(w_gate, w_up, w_down))
    masters, piece = call(
        merge_kernel, (own, swap(send)), [on_chip((ROWS, DH), f32), on_chip((ROWS, DH))]
    )
    piece, tokens = lax.optimization_barrier(
        (piece, (queries, key_vectors, value_vectors, step_rates))
    )
    pair, single = on_chip((2, BLK, DH)), on_chip((BLK, DH))
    got = call(
        tokens_kernel,
        (),
        [pair, pair, single, single] * 2 + [on_chip((2, DH), f32), on_chip((2, BLK), f32)],
        scalars=(counts,),
        hbm=(*tokens, out_gain),
        limit=16,
    )
    ke, q = got[0:2], got[2:4]
    ke_other = [swap(v) for v in got[4:6]]
    q_other = [swap(v) for v in got[6:8]]

    stacks = gather_rows(piece)
    sends, _ = update(stacks, ke[0], ke_other[0], False)
    piece, masters = renorm(masters, *scatter_rows(sends))
    stacks = gather_rows(piece)
    sends, weights = update(stacks, ke[1], ke_other[1], True)
    o0, o0_send, sq0 = apply(q[0], q_other[0], weights, True)
    r0 = swap(o0_send)
    piece, own, send = renorm(masters, *scatter_rows(sends), last=True)
    stacks = gather_rows(piece)
    finals = call(
        final_kernel,
        (own, swap(send)),
        [
            jax.ShapeDtypeStruct((2, 16, DH), f32),
            jax.ShapeDtypeStruct((2, 16, DH), f32),
            jax.ShapeDtypeStruct((2, 8, FH), f32),
        ],
    )
    stacks[0], finals = lax.optimization_barrier((stacks[0], finals))
    o1, o1_send, sq1 = apply(q[1], q_other[1], stacks, False)
    sq = jnp.concatenate([sq0, sq1], axis=1)
    total = head_sum(sq[0] + swap(sq[1]))
    r1 = swap(o1_send)
    (mixed,) = call(
        finish_kernel,
        (o0, r0, o1, r1, total, got[8], got[9]),
        [jax.ShapeDtypeStruct((2, 2, BLK, DH), bf16)],
    )
    return (mixed, *finals)


def solution(mesh):
    grid = Mesh(mesh.devices.reshape(2, 4, NX, NZ, 2), ("hz", "hy", "tx", "tz", "core"))
    head, tok = ("hz", "hy"), ("tx", "tz", "core")
    tokens = P(None, head, tok, None)
    rows = P(head, tok, None)
    return jax.shard_map(
        on_device,
        mesh=grid,
        in_specs=(tokens, tokens, tokens, P(None, head, tok), P(), P(head, None), rows, rows, rows),
        out_specs=(tokens, rows, rows, rows),
        check_vma=False,
    )
```

```python
import functools

import jax
import jax.numpy as jnp
from jax import lax
from jax.experimental import pallas as pl
from jax.experimental.pallas import tpu as pltpu
from jax.sharding import Mesh, PartitionSpec as P

HEADS = 16
DH = 256
FH = 512
BLK = 256
EPS = 1e-06
NX = 4
NZ = 4
ROWS = 96

VMEM = pl.BlockSpec(memory_space=pltpu.VMEM)
SMEM = pl.BlockSpec(memory_space=pltpu.SMEM)
NT = (((1,), (1,)), ((), ()))
NN = (((1,), (0,)), ((), ()))
f32 = jnp.float32
bf16 = jnp.bfloat16


def on_chip(shape, dtype=bf16):
    return pltpu.VMEM(shape, dtype)


def call(kernel, operands, outs, scalars=(), hbm=(), scratch=(), limit=8):
    held = [pltpu.with_memory_space_constraint(v, pltpu.VMEM) for v in operands]
    hbm = [pltpu.with_memory_space_constraint(v, pltpu.HBM) for v in hbm]
    return pl.pallas_call(
        kernel,
        in_specs=[SMEM] * len(scalars) + [VMEM] * (len(held) + len(hbm)),
        out_specs=[VMEM] * len(outs),
        out_shape=list(outs),
        scratch_shapes=list(scratch),
        compiler_params=pltpu.CompilerParams(vmem_limit_bytes=limit << 20),
    )(*scalars, *held, *hbm)


def position():
    return lax.axis_index("tx"), lax.axis_index("tz"), lax.axis_index("core")


def shift(array, axis, d):
    pairs = []
    for i in range(4):
        pairs += [(2 * i, 2 * (i ^ d)), (2 * i + 1, 2 * (i ^ ((4 - d) % 4)) + 1)]
    return lax.ppermute(array, (axis, "core"), pairs)


SWAP = [(0, 1), (1, 0)]


def mm(a, b, dims=NN):
    return lax.dot_general(a, b, dims, preferred_element_type=f32)


def chip_index(dx, dz):
    tx, tz, core = position()
    px = jnp.bitwise_xor(tx, jnp.where(core == 0, dx, (4 - dx) % 4))
    pz = jnp.bitwise_xor(tz, jnp.where(core == 0, dz, (4 - dz) % 4))
    return px * NZ + pz


def assemble(stacks, g_ref, u_ref, d_ref):
    for dx in range(NX):
        for dz in range(NZ):
            p = chip_index(dx, dz)
            f0 = pl.multiple_of(p * 32, 32)
            d0 = pl.multiple_of(p * 16, 16)
            g_ref[pl.ds(f0, 32), :] = stacks[dx][dz, 0:32, :]
            u_ref[pl.ds(f0, 32), :] = stacks[dx][dz, 32:64, :]
            d_ref[pl.ds(d0, 16), 0:256] = stacks[dx][dz, 64:80, :]
            d_ref[pl.ds(d0, 16), 256:512] = stacks[dx][dz, 80:96, :]


def split_kernel(wg, wu, wd, own, send):
    core = position()[2]
    for head, out in ((core, own), (1 - core, send)):
        out[0:16, :] = wg[head]
        out[16:32, :] = wu[head]
        out[32:40, :] = wd[head, :, 0:256]
        out[40:48, :] = wd[head, :, 256:512]


def merge_kernel(own, recv, w, piece):
    first = position()[2] == 0
    mine, theirs = own[...], recv[...]
    low = jnp.where(first, mine, theirs)
    high = jnp.where(first, theirs, mine)
    for row, size, to in ((0, 16, 0), (16, 16, 32), (32, 8, 64), (40, 8, 80)):
        w[to : to + size, :] = low[row : row + size]
        w[to + size : to + 2 * size, :] = high[row : row + size]
    piece[...] = w[...].astype(bf16)


def final_kernel(own, recv, wg, wu, wd):
    core = position()[2]
    for head, rows in ((core, own), (1 - core, recv)):
        wg[head] = rows[0:16, :]
        wu[head] = rows[16:32, :]
        wd[head, :, 0:256] = rows[32:40, :]
        wd[head, :, 256:512] = rows[40:48, :]


def tokens_kernel(counts, queries, keys, values, rates, gain_in, *outs):
    outs[8][...] = gain_in[...]
    masks = outs[9]
    ke_own, q_own, ke_out, q_out = outs[0:2], outs[2:4], outs[4:6], outs[6:8]
    tx, tz, core = position()
    tok = (tx * NZ + tz) * 2 + core
    grad_scale = float(2 * NX * NZ * BLK) ** (-0.5)
    lane = lax.broadcasted_iota(jnp.int32, (1, BLK), 1)
    for head, sends in ((core, False), (1 - core, True)):
        for g in range(2):
            valid = (lane < counts[g, tok]).astype(f32)
            masks[g : g + 1, :] = valid
            both = rates[g].astype(f32)
            row = jnp.where(head == 0, both[0:1], both[1:2]) * grad_scale * valid
            col = jnp.broadcast_to(row, (128, BLK)).T
            col = jnp.concatenate([col, col], axis=1)
            e = (values[g, head].astype(f32) * col).astype(bf16)
            ke, q = (ke_out[g], q_out[g]) if sends else (ke_own[g], q_own[g])
            ke[0], ke[1], q[...] = keys[g, head], e, queries[g, head]


def update_kernel(
    ke, ke_other, s0, s1, s2, s3, own, o1, o2, o3, g_ref, u_ref, d_ref,
    dt_ref, k_ref, e_ref, et_ref, dg_ref, du_ref, dd_ref,
):
    assemble((s0, s1, s2, s3), g_ref, u_ref, d_ref)
    k_ref[0:BLK, :] = ke[0]
    k_ref[BLK:, :] = ke_other[0]
    e_ref[0:BLK, :] = ke[1]
    e_ref[BLK:, :] = ke_other[1]
    dt_ref[...] = d_ref[...].T
    et_ref[...] = e_ref[...].T
    a = mm(g_ref[...], k_ref[...], NT)
    b = mm(u_ref[...], k_ref[...], NT)
    r = mm(dt_ref[...], e_ref[...], NT)
    s = jax.nn.sigmoid(a)
    act = a * s
    hid = (act * b).astype(bf16)
    da = (r * b * s * (1.0 + a * (1.0 - s))).astype(bf16)
    db = (r * act).astype(bf16)
    dg_ref[...] = mm(da, k_ref[...])
    du_ref[...] = mm(db, k_ref[...])
    dd_ref[...] = mm(et_ref[...], hid, NT)
    for dx, out in enumerate((own, o1, o2, o3)):
        for dz in range(NZ):
            p = chip_index(dx, dz)
            f0 = pl.multiple_of(p * 32, 32)
            d0 = pl.multiple_of(p * 16, 16)
            out[dz, 0:32, :] = dg_ref[pl.ds(f0, 32), :].astype(out.dtype)
            out[dz, 32:64, :] = du_ref[pl.ds(f0, 32), :].astype(out.dtype)
            out[dz, 64:80, :] = dd_ref[pl.ds(d0, 16), 0:256].astype(out.dtype)
            out[dz, 80:96, :] = dd_ref[pl.ds(d0, 16), 256:512].astype(out.dtype)


WEIGHTS = (((FH, DH), bf16), ((FH, DH), bf16), ((DH, FH), bf16))


def update(stacks, ke, ke_other, keep):
    weights = [on_chip(*w) for w in WEIGHTS]
    outs = [on_chip((NZ, ROWS, DH), f32)] + [on_chip((NZ, ROWS, DH))] * 3
    scratch = [
        pltpu.VMEM((FH, DH), bf16),
        pltpu.VMEM((2 * BLK, DH), bf16),
        pltpu.VMEM((2 * BLK, DH), bf16),
        pltpu.VMEM((DH, 2 * BLK), bf16),
        pltpu.VMEM((FH, DH), f32),
        pltpu.VMEM((FH, DH), f32),
        pltpu.VMEM((DH, FH), f32),
    ]
    operands = (ke, ke_other, *stacks)
    if keep:
        got = call(update_kernel, operands, outs + weights, scratch=scratch, limit=20)
        return got[:4], got[4:]
    return call(update_kernel, operands, outs, scratch=weights + scratch, limit=20), None


def partial_kernel(own, r1, r2, r3, y0, y1, y2, y3):
    for dz, out in enumerate((y0, y1, y2, y3)):
        total = own[dz] + r1[dz].astype(f32) + r2[dz].astype(f32) + r3[dz].astype(f32)
        out[...] = total.astype(out.dtype)


def partial_sum(own, recv):
    return call(
        partial_kernel, (own, *recv), [on_chip((ROWS, DH), f32)] + [on_chip((ROWS, DH))] * 3
    )


def renorm_kernel(w, y0, t1, t2, t3, piece, *outs, last):
    old = w[...]
    new = old + (y0[...] + t1[...].astype(f32) + t2[...].astype(f32) + t3[...].astype(f32))

    def mean_square(v):
        sums = jnp.sum(v * v, axis=-1, keepdims=True)
        wide = (sums[64:80] + sums[80:96]) * (1.0 / FH)
        return jnp.concatenate([sums[0:64] * (1.0 / DH), wide, wide], axis=0)

    scaled = new * jnp.sqrt(mean_square(old)) * lax.rsqrt(mean_square(new) + EPS)
    piece[...] = scaled.astype(bf16)
    if not last:
        outs[0][...] = scaled
        return
    first = position()[2] == 0
    for row, size, at in ((0, 16, 0), (16, 16, 32), (32, 8, 64), (40, 8, 80)):
        low = scaled[at : at + size, :]
        high = scaled[at + size : at + 2 * size, :]
        outs[0][row : row + size, :] = jnp.where(first, low, high)
        outs[1][row : row + size, :] = jnp.where(first, high, low)


def renorm(w, y0, recv, last=False):
    held = [on_chip((48, DH), f32)] * 2 if last else [on_chip((ROWS, DH), f32)]
    return call(
        functools.partial(renorm_kernel, last=last), (w, y0, *recv), [on_chip((ROWS, DH)), *held]
    )


def apply_kernel(q, q_other, *refs, assembled):
    if assembled:
        g_ref, u_ref, d_ref, o_own, o_send, sq = refs
    else:
        o_own, o_send, sq, g_ref, u_ref, d_ref = refs[4:]
        assemble(refs[:4], g_ref, u_ref, d_ref)
    query = jnp.concatenate([q[...], q_other[...]], axis=0)
    a = mm(query, g_ref[...], NT)
    b = mm(query, u_ref[...], NT)
    hid = (a * jax.nn.sigmoid(a) * b).astype(bf16)
    o = mm(hid, d_ref[...], NT)
    o_own[...] = o[0:BLK]
    o_send[...] = o[BLK:].astype(bf16)
    sums = jnp.broadcast_to(jnp.sum(o * o, axis=-1, keepdims=True), (2 * BLK, 128)).T
    sq[0] = sums[0:4, 0:BLK]
    sq[1] = sums[0:4, BLK:]


def apply(q, q_other, weights, assembled):
    return call(
        functools.partial(apply_kernel, assembled=assembled),
        (q, q_other, *weights),
        [on_chip((BLK, DH), f32), on_chip((BLK, DH)), on_chip((2, 4, BLK), f32)],
        scratch=() if assembled else [pltpu.VMEM(*w) for w in WEIGHTS],
        limit=16,
    )


def finish_kernel(o0, r0, o1, r1, sq, gain, masks, out):
    core = position()[2]
    for g, (own, other) in enumerate(((o0, r0), (o1, r1))):
        row = lax.rsqrt(sq[4 * g : 4 * g + 1, :] * (1.0 / (HEADS * DH)) + EPS)
        scale = jnp.broadcast_to(row * masks[g : g + 1, :], (128, BLK)).T
        scale = jnp.concatenate([scale, scale], axis=1)
        for head, o in ((core, own), (1 - core, other)):
            out[g, head] = (o[...].astype(f32) * gain[pl.ds(head, 1), :] * scale).astype(bf16)


def gather_rows(piece):
    parts = [piece] + [shift(piece, "tz", d) for d in (1, 2, 3)]
    stack = jnp.stack(parts)
    return [stack] + [shift(stack, "tx", d) for d in (1, 2, 3)]


def scatter_rows(sends):
    recv = [shift(sends[d], "tx", d) for d in (1, 2, 3)]
    y = partial_sum(sends[0], recv)
    return y[0], [shift(y[d], "tz", d) for d in (1, 2, 3)]


def head_sum(sq):
    sq = sq + sum(shift(sq, "hy", d) for d in (1, 2, 3))
    return sq + lax.ppermute(sq, "hz", SWAP)


def swap(array):
    return lax.ppermute(array, "core", SWAP)


def on_device(
    queries, key_vectors, value_vectors, step_rates, counts, out_gain, w_gate, w_up, w_down
):
    half = on_chip((48, DH), f32)
    own, send = call(split_kernel, (), [half, half], hbm=(w_gate, w_up, w_down))
    masters, piece = call(
        merge_kernel, (own, swap(send)), [on_chip((ROWS, DH), f32), on_chip((ROWS, DH))]
    )
    piece, tokens = lax.optimization_barrier(
        (piece, (queries, key_vectors, value_vectors, step_rates))
    )
    pair, single = on_chip((2, BLK, DH)), on_chip((BLK, DH))
    got = call(
        tokens_kernel,
        (),
        [pair, pair, single, single] * 2 + [on_chip((2, DH), f32), on_chip((2, BLK), f32)],
        scalars=(counts,),
        hbm=(*tokens, out_gain),
        limit=16,
    )
    ke, q = got[0:2], got[2:4]
    ke_other = [swap(v) for v in got[4:6]]
    q_other = [swap(v) for v in got[6:8]]

    stacks = gather_rows(piece)
    sends, _ = update(stacks, ke[0], ke_other[0], False)
    piece, masters = renorm(masters, *scatter_rows(sends))
    stacks = gather_rows(piece)
    sends, weights = update(stacks, ke[1], ke_other[1], True)
    o0, o0_send, sq0 = apply(q[0], q_other[0], weights, True)
    r0 = swap(o0_send)
    piece, own, send = renorm(masters, *scatter_rows(sends), last=True)
    stacks = gather_rows(piece)
    finals = call(
        final_kernel,
        (own, swap(send)),
        [
            jax.ShapeDtypeStruct((2, 16, DH), f32),
            jax.ShapeDtypeStruct((2, 16, DH), f32),
            jax.ShapeDtypeStruct((2, 8, FH), f32),
        ],
    )
    stacks[0], finals = lax.optimization_barrier((stacks[0], finals))
    o1, o1_send, sq1 = apply(q[1], q_other[1], stacks, False)
    sq = jnp.concatenate([sq0, sq1], axis=1)
    total = head_sum(sq[0] + swap(sq[1]))
    r1 = swap(o1_send)
    (mixed,) = call(
        finish_kernel,
        (o0, r0, o1, r1, total, got[8], got[9]),
        [jax.ShapeDtypeStruct((2, 2, BLK, DH), bf16)],
    )
    return (mixed, *finals)


def solution(mesh):
    grid = Mesh(mesh.devices.reshape(2, 4, NX, NZ, 2), ("hz", "hy", "tx", "tz", "core"))
    head, tok = ("hz", "hy"), ("tx", "tz", "core")
    tokens = P(None, head, tok, None)
    rows = P(head, tok, None)
    return jax.shard_map(
        on_device,
        mesh=grid,
        in_specs=(tokens, tokens, tokens, P(None, head, tok), P(), P(head, None), rows, rows, rows),
        out_specs=(tokens, rows, rows, rows),
        check_vma=False,
    )
```
